256 devices in a mesh: row: 8 (over z), col: 16 (over x_hi, y, core), rep: 2 (over x_lo).
Axes of the slice: x: 4 (x_hi: 2, x_lo: 2; x = x_hi * 2 + x_lo), y: 4, z: 8, core: 2. Of those that a mesh axis runs over, the one named last changes fastest.
Arguments:
- amplitudes: bfloat16 [8192, 8192], P('row', 'col'), may hold values from -6 to 6
- intermediate: bfloat16 [8192, 8192], P('row', 'col'), may hold values from -0.0625 to 0.0625
Outputs:
- residual: float32 [16, 16, 32, 8192], P(None, 'col', None, ('row', 'rep'))
The draws below stay inside these ranges and needn't reach their ends.
All inputs are finite; a program needn't handle non-finite values.
Results may differ from the reference program's by a relative error of at most 0.0029.
Values may be sent and summed in bfloat16 or wider, within the bound.
No kernel may reach another device: no remote copies, remote signals or barrier semaphores. Data moves between devices by JAX's collectives and lax.ppermute only.
A program may use at most 128 MiB of HBM per device.

```python
import jax
import jax.numpy as jnp

KC_WIDTH = 8192
PAIR_DEV = 32
PAIRS = 8192
N_ROW = 8
N_COL = 16
N_REP = 2


def block_levels(rng, shape, cuts, least, largest):
    def one(dim, blocks):
        heights = jax.random.uniform(jax.random.fold_in(jax.random.fold_in(rng, 6), dim), (blocks,), jnp.float32, least / len(cuts), largest / len(cuts))
        return jnp.repeat(jnp.exp(heights), shape[dim] // blocks).reshape((-1,) + (1,) * (len(shape) - dim - 1))

    loudness = one(*cuts[0])
    for cut in cuts[1:]:
        loudness = loudness * one(*cut)
    return loudness


def scatter_about(stream_key, dims, width, bound, split=(), held_as=jnp.bfloat16):
    values = jax.random.normal(stream_key, dims, jnp.float32) * width
    if len(split) > 0:
        values = block_levels(stream_key, dims, split, -0.22, 0.18) * values
    return jnp.clip(values, min=-bound, max=bound).astype(held_as)


def setup_inputs(seed: int = 0) -> dict:
    keys = jax.random.split(jax.random.key(seed), 3)
    return {
        "amplitudes": scatter_about(keys[0], (PAIRS, KC_WIDTH), 1.0, 6.0, ((0, 8), (1, 16))),
        "intermediate": scatter_about(keys[1], (KC_WIDTH, PAIRS), KC_WIDTH ** -0.5, 0.0625, ((0, 8), (1, 16))),
    }


def reference(amplitudes, intermediate):
    cycle = jnp.dot(amplitudes, intermediate, preferred_element_type=jnp.float32).astype(jnp.bfloat16)
    widened = cycle.astype(jnp.float32)
    symmetric = widened + widened.T
    return symmetric.reshape(N_ROW * N_REP, N_COL, PAIR_DEV, PAIRS)
```

```python
import functools

import jax
import jax.numpy as jnp
import numpy as np
from jax import lax
from jax.experimental import pallas as pl
from jax.experimental.pallas import tpu as pltpu
from jax.sharding import Mesh, PartitionSpec as P

AXES = ("row", "xh", "y", "core", "rep")
F32, BF16 = jnp.float32, jnp.bfloat16
X_LINE = ("xh", "rep")
PAIR = [(0, 1), (1, 0), (2, 3), (3, 2)]
CROSS = [(0, 3), (3, 0), (1, 2), (2, 1)]
B = 512


def call(body, outs, n_scalar, n_in, flops=0, moved=0, scratch=()):
    vmem = pl.BlockSpec(memory_space=pltpu.VMEM)
    smem = pl.BlockSpec(memory_space=pltpu.SMEM)
    return pl.pallas_call(
        body,
        out_shape=outs,
        in_specs=[smem] * n_scalar + [vmem] * n_in,
        out_specs=[vmem] * len(outs),
        scratch_shapes=list(scratch),
        compiler_params=pltpu.CompilerParams(vmem_limit_bytes=48 << 20),
        cost_estimate=pl.CostEstimate(flops=flops, bytes_accessed=moved, transcendentals=0),
    )


def lane_block(shape):
    return lax.broadcasted_iota(jnp.int32, shape, len(shape) - 1) // 32


def turn(parts):
    block = lane_block(parts[0].shape)
    out = []
    for j in range(4):
        rolled = [pltpu.roll(p, ((i - j) * 32) % 128, 1) if i != j else p for i, p in enumerate(parts)]
        out.append(
            jnp.where(
                block < 2, jnp.where(block == 0, rolled[0], rolled[1]), jnp.where(block == 2, rolled[2], rolled[3])
            )
        )
    return out


def w_pack(rep_ref, w_ref, out_ref):
    rep = rep_ref[0]
    for half in range(2):
        for g in range(4):
            parts = []
            for hi in range(4):
                v = w_ref[half * B + hi * 128 : half * B + (hi + 1) * 128, g * 128 : (g + 1) * 128].astype(F32)
                parts.append(jnp.where(rep == 0, v, pltpu.roll(v, 96, 1)))
            turned = turn(parts)
            for j in (0, 2):
                out_ref[g * 2 + j // 2, half] = turned[j].astype(BF16)


def w_unpack(in_ref, out_ref):
    for g in range(4):
        turned = turn([in_ref[4 * g + j].astype(F32) for j in range(4)])
        for hi in range(4):
            out_ref[hi * 128 : (hi + 1) * 128, g * 128 : (g + 1) * 128] = turned[hi].astype(BF16)


def dot(a, b):
    return jnp.dot(a, b, preferred_element_type=F32)


def product_early(slots, pos_ref, w_ref, *refs):
    pieces, (first_ref, second_ref) = refs[: len(slots)], refs[len(slots) :]
    for which, out_ref in ((0, first_ref), (1, second_ref)):
        total = None
        for (half, p), piece in zip(slots, pieces):
            if half == which:
                term = dot(piece[...], w_ref[pos_ref[p]])
                total = term if total is None else total + term
        out_ref[...] = total


def product_late(early, late, pos_ref, keep_ref, first_in, second_in, w_ref, top_ref, bottom_ref, *refs):
    old, new = refs[: len(early)], refs[len(early) : len(early) + len(late)]
    kept_ref, sent_ref, far_ref, sums = refs[len(early) + len(late) :]
    far_ref[:256] = top_ref[...]
    far_ref[256:] = bottom_ref[...]
    sums[0] = first_in[...]
    sums[1] = second_in[...]
    for (half, p), piece in zip(early, old):

        @pl.when(pos_ref[p] == 4)
        def _(half=half, piece=piece):
            sums[half] += dot(piece[...], far_ref[...])

    for (half, p), piece in zip(late, new):

        @pl.when(pos_ref[p] == 4)
        def _(half=half, piece=piece):
            sums[half] += dot(piece[...], far_ref[...])

        @pl.when(pos_ref[p] != 4)
        def _(half=half, p=p, piece=piece):
            sums[half] += dot(piece[...], w_ref[pos_ref[p]])

    keep = keep_ref[0]
    kept_ref[...] = sums[keep]
    sent_ref[...] = sums[1 - keep]


def spread(kept_ref, got_ref, direct_ref, mirror_ref):
    cycle = (kept_ref[...] + got_ref[...]).astype(BF16).astype(F32)
    direct_ref[...] = cycle.T.astype(BF16)
    split = cycle.reshape(16, 4, 8, B)
    for g in range(4):
        parts = [split[:, hi, :, g * 128 : (g + 1) * 128].reshape(128, 128) for hi in range(4)]
        for j, t in enumerate(turn(parts)):
            mirror_ref[2 * g + j // 2, :, j % 2] = t.reshape(16, 8, 128).astype(BF16)


def finish(direct_ref, mirror_ref, out_ref):
    for owner in range(16):
        z, core = owner // 2, owner % 2
        for g in range(4):
            parts = [mirror_ref[z, 2 * g + j // 2, core, j % 2].astype(F32) for j in range(4)]
            for hi, t in enumerate(turn(parts)):
                rows = slice(owner * 32 + hi * 8, owner * 32 + hi * 8 + 8)
                lanes = slice(g * 128, (g + 1) * 128)
                out_ref[rows, lanes] = t + direct_ref[rows, lanes].astype(F32)


def ring(n, step):
    return [(i, (i + step) % n) for i in range(n)]


def after(x, *others):
    return lax.optimization_barrier((x, *others))[0]


def local(amplitudes, intermediate):
    z, xh, y, core, rep = (lax.axis_index(a) for a in AXES)
    shape = jax.ShapeDtypeStruct
    up = lambda v, axis, n: lax.ppermute(v, axis, ring(n, -1))
    down = lambda v, axis, n: lax.ppermute(v, axis, ring(n, 1))
    pair = lambda v: lax.ppermute(v, X_LINE, PAIR)
    cross = lambda v: lax.ppermute(v, X_LINE, CROSS)

    packed = call(w_pack, [shape((8, 2, 128, 128), BF16)], 1, 1, moved=2 << 20)(
        rep.reshape(1).astype(jnp.int32), intermediate
    )[0]
    arrived = lax.all_to_all(packed.reshape(16, 128, 128), ("xh", "y", "core"), split_axis=0, concat_axis=0, tiled=True)
    w = {0: call(w_unpack, [shape((B, B), BF16)], 0, 1, moved=1 << 20)(arrived)[0]}

    f = {(0, 0): lax.dynamic_slice_in_dim(amplitudes, rep * B, B, 0)}
    g = {(0, 0): lax.dynamic_slice_in_dim(amplitudes, (1 - rep) * B, B, 0)}
    f[0, 1] = up(f[0, 0], "y", 4)
    f[0, 3] = down(f[0, 0], "y", 4)
    f[1, 0] = cross(g[0, 0])
    w[1], w[7] = up(w[0], "row", 8), down(w[0], "row", 8)
    f[0, 2] = up(f[0, 1], "y", 4)
    f[1, 3] = down(f[1, 0], "y", 4)
    g[0, 1] = pair(f[0, 1])
    g[1, 0] = cross(after(f[0, 0], f[1, 0]))
    w[2], w[6] = up(w[1], "row", 8), down(w[7], "row", 8)
    f[1, 1] = up(after(f[1, 0], f[0, 2]), "y", 4)
    f[1, 2] = down(f[1, 3], "y", 4)
    g[0, 3] = pair(after(f[0, 3], g[0, 1]))
    g[1, 1] = cross(after(f[0, 1], g[1, 0]))
    w[3], w[5] = up(w[2], "row", 8), down(w[6], "row", 8)
    g[0, 2] = pair(after(f[0, 2], g[0, 3]))
    g[1, 2] = cross(after(f[0, 2], g[1, 1]))
    g[1, 3] = down(after(g[1, 0], f[1, 2]), "y", 4)
    top, bottom = up(w[3][:256], "row", 8), down(w[5][256:], "row", 8)

    spots = [(i, j) for i in range(2) for j in range(4)]
    position = jnp.stack(
        [(4 * lax.rem(xh + i, 2) + lax.rem(y + j, 4) - z + 8) % 8 for i, j in spots]
    ).astype(jnp.int32)
    late = [(1, spots.index(s)) for s in ((0, 2), (1, 2), (1, 3))]
    early = [(h, p) for h in range(2) for p in range(8) if (h, p) not in late]
    piece = lambda h, p: (f, g)[h][spots[p]]
    stack = jnp.stack([w[0], w[1], w[2], w[3], jnp.zeros((B, B), BF16), w[5], w[6], w[7]])
    old = [piece(*e) for e in early]
    first, second = call(
        functools.partial(product_early, early),
        [shape((B, B), F32)] * 2,
        1,
        1 + len(early),
        flops=2 * B**3 * len(early),
        moved=12 << 20,
    )(position, stack, *old)
    kept, sent = call(
        functools.partial(product_late, early, late),
        [shape((B, B), F32)] * 2,
        2,
        5 + 16,
        flops=2 * B**3 * 5,
        moved=8 << 20,
        scratch=[pltpu.VMEM((B, B), BF16), pltpu.VMEM((2, B, B), F32)],
    )(
        position,
        (core ^ rep).reshape(1).astype(jnp.int32),
        first,
        second,
        stack,
        top,
        bottom,
        *old,
        *[piece(*e) for e in late],
    )
    got = lax.ppermute(sent, "core", [(0, 1), (1, 0)])
    direct, mirror = call(
        spread, [shape((B, B), BF16), shape((8, 16, 2, 8, 128), BF16)], 0, 2, moved=3 << 20
    )(kept, got)
    direct = lax.ppermute(direct, ("core", "rep"), [(0, 0), (1, 2), (2, 1), (3, 3)])
    mirror = lax.all_to_all(mirror.reshape(256, 8, 128), AXES, split_axis=0, concat_axis=0, tiled=True)
    out = call(finish, [shape((B, B), F32)], 0, 2, moved=2 << 20)(direct, mirror.reshape(8, 8, 2, 2, 8, 128))[0]
    return out.reshape(16, 1, 32, B)


def solution(mesh):
    fine = Mesh(np.asarray(mesh.devices).reshape(8, 2, 4, 2, 2), AXES)
    block = P("row", ("xh", "y", "core"))
    out = P(None, ("xh", "y", "core"), None, ("row", "rep"))
    return jax.shard_map(local, mesh=fine, in_specs=(block, block), out_specs=out, check_vma=False)
```

```python
import jax
import jax.numpy as jnp
import numpy as np
from jax import lax
from jax.experimental import pallas as pl
from jax.experimental.pallas import tpu as pltpu
from jax.sharding import Mesh, PartitionSpec as P

AXES = ("row", "xh", "y", "core", "rep")
F32, BF16 = jnp.float32, jnp.bfloat16
X_LINE = ("xh", "rep")
PAIR = [(0, 1), (1, 0), (2, 3), (3, 2)]
CROSS = [(0, 3), (3, 0), (1, 2), (2, 1)]
B = 512


def call(body, outs, n_scalar, n_in, flops=0, moved=0, scratch=(), limit=20):
    vmem = pl.BlockSpec(memory_space=pltpu.VMEM)
    smem = pl.BlockSpec(memory_space=pltpu.SMEM)
    return pl.pallas_call(
        body,
        out_shape=outs,
        in_specs=[smem] * n_scalar + [vmem] * n_in,
        out_specs=[vmem] * len(outs),
        scratch_shapes=list(scratch),
        compiler_params=pltpu.CompilerParams(vmem_limit_bytes=limit << 20),
        cost_estimate=pl.CostEstimate(flops=flops, bytes_accessed=moved, transcendentals=0),
    )


def lane_block(shape):
    return lax.broadcasted_iota(jnp.int32, shape, len(shape) - 1) // 32


def turn(parts):
    block = lane_block(parts[0].shape)
    out = []
    for j in range(4):
        rolled = [pltpu.roll(p, ((i - j) * 32) % 128, 1) if i != j else p for i, p in enumerate(parts)]
        out.append(
            jnp.where(
                block < 2, jnp.where(block == 0, rolled[0], rolled[1]), jnp.where(block == 2, rolled[2], rolled[3])
            )
        )
    return out


def w_pack(rep_ref, w_ref, out_ref):
    rep = rep_ref[0]
    for half in range(2):
        for g in range(4):
            parts = []
            for hi in range(4):
                v = w_ref[half * B + hi * 128 : half * B + (hi + 1) * 128, g * 128 : (g + 1) * 128].astype(F32)
                parts.append(jnp.where(rep == 0, v, pltpu.roll(v, 96, 1)))
            turned = turn(parts)
            for j in (0, 2):
                out_ref[g * 2 + j // 2, half] = turned[j].astype(BF16)


def w_unpack(in_ref, out_ref):
    for g in range(4):
        turned = turn([in_ref[4 * g + j].astype(F32) for j in range(4)])
        for hi in range(4):
            out_ref[hi * 128 : (hi + 1) * 128, g * 128 : (g + 1) * 128] = turned[hi].astype(BF16)


def dot(a, b):
    return jnp.dot(a, b, preferred_element_type=F32)


def product_early(pos_ref, w_ref, *refs):
    for half in range(2):
        total = None
        for p in range(8):
            term = dot(refs[half * 8 + p][...], w_ref[pos_ref[p]])
            total = term if total is None else total + term
        refs[16 + half][...] = total


def product_late(pos_ref, keep_ref, first_ref, second_ref, top_ref, bottom_ref, *refs):
    kept_ref, sent_ref, far_ref = refs[16:]
    far_ref[:256] = top_ref[...]
    far_ref[256:] = bottom_ref[...]
    first_kept = keep_ref[0] == 0
    for p in range(8):

        @pl.when(pos_ref[p] == 4)
        def _(p=p):
            first = first_ref[...] + dot(refs[p][...], far_ref[...])
            second = second_ref[...] + dot(refs[8 + p][...], far_ref[...])
            kept_ref[...] = jnp.where(first_kept, first, second)
            sent_ref[...] = jnp.where(first_kept, second, first)


def spread(kept_ref, got_ref, direct_ref, mirror_ref):
    cycle = (kept_ref[...] + got_ref[...]).astype(BF16).astype(F32)
    direct_ref[...] = cycle.T.astype(BF16)
    split = cycle.reshape(16, 4, 8, B)
    for g in range(4):
        parts = [split[:, hi, :, g * 128 : (g + 1) * 128].reshape(128, 128) for hi in range(4)]
        for j, t in enumerate(turn(parts)):
            mirror_ref[2 * g + j // 2, :, j % 2] = t.reshape(16, 8, 128).astype(BF16)


def finish(direct_ref, mirror_ref, out_ref):
    for owner in range(16):
        z, core = owner // 2, owner % 2
        for g in range(4):
            parts = [mirror_ref[z, 2 * g + j // 2, core, j % 2].astype(F32) for j in range(4)]
            for hi, t in enumerate(turn(parts)):
                rows = slice(owner * 32 + hi * 8, owner * 32 + hi * 8 + 8)
                lanes = slice(g * 128, (g + 1) * 128)
                out_ref[rows, lanes] = t + direct_ref[rows, lanes].astype(F32)


def ring(n, step):
    return [(i, (i + step) % n) for i in range(n)]


def lockstep(*groups):
    return lax.optimization_barrier(groups)


def local(amplitudes, intermediate):
    z, xh, y, core, rep = (lax.axis_index(a) for a in AXES)
    shape = jax.ShapeDtypeStruct
    up = lambda v, axis, n: lax.ppermute(v, axis, ring(n, -1))
    down = lambda v, axis, n: lax.ppermute(v, axis, ring(n, 1))
    pair = lambda v: lax.ppermute(v, X_LINE, PAIR)
    cross = lambda v: lax.ppermute(v, X_LINE, CROSS)

    f00 = lax.dynamic_slice_in_dim(amplitudes, rep * B, B, 0)
    g00 = lax.dynamic_slice_in_dim(amplitudes, (1 - rep) * B, B, 0)
    f01, f03, f10 = up(f00, "y", 4), down(f00, "y", 4), cross(g00)

    intermediate, f00, g00 = lax.optimization_barrier((intermediate, f00, g00))
    packed = call(w_pack, [shape((8, 2, 128, 128), BF16)], 1, 1, moved=2 << 20)(
        rep.reshape(1).astype(jnp.int32), intermediate
    )[0]
    arrived = lax.all_to_all(packed.reshape(16, 128, 128), ("xh", "y", "core"), split_axis=0, concat_axis=0, tiled=True)
    w0 = call(w_unpack, [shape((B, B), BF16)], 0, 1, moved=1 << 20)(arrived)[0]

    w0, f00, f01, f03, f10 = lockstep(w0, f00, f01, f03, f10)
    w1, w7 = up(w0, "row", 8), down(w0, "row", 8)
    f02, f13, g01, g10 = up(f01, "y", 4), down(f10, "y", 4), pair(f01), cross(f00)

    w1, w7, f02, f13, g01, g10, f10, f03, f01 = lockstep(w1, w7, f02, f13, g01, g10, f10, f03, f01)
    w2, w6 = up(w1, "row", 8), down(w7, "row", 8)
    f11, f12, g03, g11 = up(f10, "y", 4), down(f13, "y", 4), pair(f03), cross(f01)

    w2, w6, f11, f12, g03, g11, f02, g10 = lockstep(w2, w6, f11, f12, g03, g11, f02, g10)
    w3, w5 = up(w2, "row", 8), down(w6, "row", 8)
    g02, g12, g13 = pair(f02), cross(f02), down(g10, "y", 4)

    w3, w5, g02, g12, g13 = lockstep(w3, w5, g02, g12, g13)
    top, bottom = up(w3[:256], "row", 8), down(w5[256:], "row", 8)

    pieces = (f00, f01, f02, f03, f10, f11, f12, f13, g00, g01, g02, g03, g10, g11, g12, g13)
    position = jnp.stack(
        [(4 * lax.rem(xh + i, 2) + lax.rem(y + j, 4) - z + 8) % 8 for i in range(2) for j in range(4)]
    ).astype(jnp.int32)
    stack = jnp.stack([w0, w1, w2, w3, jnp.zeros((B, B), BF16), w5, w6, w7])
    first, second = call(
        product_early, [shape((B, B), F32)] * 2, 1, 17, flops=32 * B**3, moved=12 << 20
    )(position, stack, *pieces)
    kept, sent = call(
        product_late,
        [shape((B, B), F32)] * 2,
        2,
        4 + 16,
        flops=4 * B**3,
        moved=4 << 20,
        scratch=[pltpu.VMEM((B, B), BF16)],
    )(position, (core ^ rep).reshape(1).astype(jnp.int32), first, second, top, bottom, *pieces)
    got = lax.ppermute(sent, "core", [(0, 1), (1, 0)])
    direct, mirror = call(
        spread, [shape((B, B), BF16), shape((8, 16, 2, 8, 128), BF16)], 0, 2, moved=3 << 20
    )(kept, got)
    direct = lax.ppermute(direct, ("core", "rep"), [(0, 0), (1, 2), (2, 1), (3, 3)])
    mirror = lax.all_to_all(mirror.reshape(256, 8, 128), AXES, split_axis=0, concat_axis=0, tiled=True)
    out = call(finish, [shape((B, B), F32)], 0, 2, moved=2 << 20)(direct, mirror.reshape(8, 8, 2, 2, 8, 128))[0]
    return out.reshape(16, 1, 32, B)


def solution(mesh):
    fine = Mesh(np.asarray(mesh.devices).reshape(8, 2, 4, 2, 2), AXES)
    block = P("row", ("xh", "y", "core"))
    out = P(None, ("xh", "y", "core"), None, ("row", "rep"))
    return jax.shard_map(local, mesh=fine, in_specs=(block, block), out_specs=out, check_vma=False)
```

```python
import jax
import jax.numpy as jnp
import numpy as np
from jax import lax
from jax.experimental import pallas as pl
from jax.experimental.pallas import tpu as pltpu
from jax.sharding import Mesh, PartitionSpec as P

AXES = ("row", "xh", "y", "core", "rep")
F32, BF16 = jnp.float32, jnp.bfloat16
X_LINE = ("xh", "rep")
PAIR = [(0, 1), (1, 0), (2, 3), (3, 2)]
CROSS = [(0, 3), (3, 0), (1, 2), (2, 1)]
B = 512


def call(body, outs, n_scalar, n_in, flops=0, moved=0, scratch=(), limit=20):
    vmem = pl.BlockSpec(memory_space=pltpu.VMEM)
    smem = pl.BlockSpec(memory_space=pltpu.SMEM)
    return pl.pallas_call(
        body,
        out_shape=outs,
        in_specs=[smem] * n_scalar + [vmem] * n_in,
        out_specs=[vmem] * len(outs),
        scratch_shapes=list(scratch),
        compiler_params=pltpu.CompilerParams(vmem_limit_bytes=limit << 20),
        cost_estimate=pl.CostEstimate(flops=flops, bytes_accessed=moved, transcendentals=0),
    )


def lane_block(shape):
    return lax.broadcasted_iota(jnp.int32, shape, len(shape) - 1) // 32


def turn(parts):
    block = lane_block(parts[0].shape)
    out = []
    for j in range(4):
        rolled = [pltpu.roll(p, ((i - j) * 32) % 128, 1) if i != j else p for i, p in enumerate(parts)]
        out.append(
            jnp.where(
                block < 2, jnp.where(block == 0, rolled[0], rolled[1]), jnp.where(block == 2, rolled[2], rolled[3])
            )
        )
    return out


def w_pack(rep_ref, w_ref, out_ref):
    rep = rep_ref[0]
    for half in range(2):
        for g in range(4):
            parts = []
            for hi in range(4):
                v = w_ref[half * B + hi * 128 : half * B + (hi + 1) * 128, g * 128 : (g + 1) * 128].astype(F32)
                parts.append(jnp.where(rep == 0, v, pltpu.roll(v, 96, 1)))
            turned = turn(parts)
            for j in (0, 2):
                out_ref[g * 2 + j // 2, half] = turned[j].astype(BF16)


def w_unpack(in_ref, out_ref):
    for g in range(4):
        turned = turn([in_ref[4 * g + j].astype(F32) for j in range(4)])
        for hi in range(4):
            out_ref[hi * 128 : (hi + 1) * 128, g * 128 : (g + 1) * 128] = turned[hi].astype(BF16)


def dot(a, b):
    return jnp.dot(a, b, preferred_element_type=F32)


def product_early(pos_ref, *refs):
    chunks, pieces, (sum_ref, far_ref, held) = refs[:7], refs[7:15], refs[15:]
    for j, chunk in zip((0, 1, 2, 3, 5, 6, 7), chunks):
        held[j] = chunk[...]
    held[4] = jnp.zeros((B, B), BF16)
    for rows in (slice(0, B), slice(B, 2 * B)):
        total = None
        for p in range(8):
            term = dot(pieces[p][rows], held[pos_ref[p]])
            total = term if total is None else total + term
        sum_ref[rows] = total
    for p in range(8):

        @pl.when(pos_ref[p] == 4)
        def _(p=p):
            far_ref[...] = pieces[p][...]


def product_late(half_ref, sum_ref, far_ref, top_ref, bottom_ref, out_ref):
    rows = pl.ds(pl.multiple_of(half_ref[0] * B, B), B)
    block = far_ref[rows, :]
    out_ref[...] = sum_ref[rows, :] + dot(block[:, : B // 2], top_ref[...]) + dot(block[:, B // 2 :], bottom_ref[...])


def spread(kept_ref, got_ref, direct_ref, mirror_ref):
    cycle = (kept_ref[...] + got_ref[...]).astype(BF16).astype(F32)
    direct_ref[...] = cycle.T.astype(BF16)
    split = cycle.reshape(16, 4, 8, B)
    for g in range(4):
        parts = [split[:, hi, :, g * 128 : (g + 1) * 128].reshape(128, 128) for hi in range(4)]
        for j, t in enumerate(turn(parts)):
            mirror_ref[2 * g + j // 2, :, j % 2] = t.reshape(16, 8, 128).astype(BF16)


def finish(direct_ref, mirror_ref, out_ref):
    for owner in range(16):
        z, core = owner // 2, owner % 2
        for g in range(4):
            parts = [mirror_ref[z, 2 * g + j // 2, core, j % 2].astype(F32) for j in range(4)]
            for hi, t in enumerate(turn(parts)):
                rows = slice(owner * 32 + hi * 8, owner * 32 + hi * 8 + 8)
                lanes = slice(g * 128, (g + 1) * 128)
                out_ref[rows, lanes] = t + direct_ref[rows, lanes].astype(F32)


def ring(n, step):
    return [(i, (i + step) % n) for i in range(n)]


def along_y(v):
    perm = []
    for y in range(4):
        for core in range(2):
            for rep in range(2):
                to = (y + (1 if core ^ rep else -1)) % 4
                perm.append(((y * 2 + core) * 2 + rep, (to * 2 + core) * 2 + rep))
    return lax.ppermute(v, ("y", "core", "rep"), perm)


def local(amplitudes, intermediate):
    z, xh, y, core, rep = (lax.axis_index(a) for a in AXES)
    shape = jax.ShapeDtypeStruct
    pair = lambda v: lax.ppermute(v, X_LINE, PAIR)
    cross = lambda v: lax.ppermute(v, X_LINE, CROSS)
    above = lambda v: lax.ppermute(v, "row", ring(8, -1))
    below = lambda v: lax.ppermute(v, "row", ring(8, 1))

    step = 1 - 2 * (core ^ rep)
    position = jnp.stack(
        [(4 * ((xh + i) % 2) + (y + j + 4) % 4 - z + 8) % 8 for i in range(2) for j in (0, step, 2, -step)]
    ).astype(jnp.int32)
    halves = jnp.stack([core, 1 - core]).astype(jnp.int32)
    rep = rep.reshape(1).astype(jnp.int32)
    position, halves, rep, intermediate, own = lax.optimization_barrier(
        (position, halves, rep, intermediate, amplitudes)
    )

    packed = call(w_pack, [shape((8, 2, 128, 128), BF16)], 1, 1, moved=2 << 20)(rep, intermediate)[0]
    arrived = lax.all_to_all(packed.reshape(16, 128, 128), ("xh", "y", "core"), split_axis=0, concat_axis=0, tiled=True)
    w0 = call(w_unpack, [shape((B, B), BF16)], 0, 1, moved=1 << 20)(arrived)[0]

    y1, c1_top = along_y(own), cross(own[:B])
    w0, y1, c1_top = lax.optimization_barrier((w0, y1, c1_top))
    w1, w7 = above(w0), below(w0)
    y2, p1, c1_bottom = along_y(y1), pair(y1), cross(own[B:])

    w1, w7, y2, c1_bottom, y1 = lax.optimization_barrier((w1, w7, y2, c1_bottom, y1))
    c1 = jnp.concatenate([c1_top, c1_bottom])
    w2, w6 = above(w1), below(w7)
    y3, c2 = along_y(c1), cross(y1)

    w2, w6, y3, p1 = lax.optimization_barrier((w2, w6, y3, p1))
    w3, w5 = above(w2), below(w6)
    y4 = along_y(y3)

    w3, w5, y4, c2 = lax.optimization_barrier((w3, w5, y4, c2))
    top, bottom = above(w3[: B // 2]), below(w5[B // 2 :])

    total, far = call(
        product_early,
        [shape((2 * B, B), F32), shape((2 * B, B), BF16)],
        1,
        15,
        flops=32 * B**3,
        moved=16 << 20,
        scratch=[pltpu.VMEM((8, B, B), BF16)],
        limit=28,
    )(position, w0, w1, w2, w3, w5, w6, w7, own, y1, y2, p1, c1, y3, y4, c2)
    late = lambda half: call(product_late, [shape((B, B), F32)], 1, 4, flops=2 * B**3, moved=4 << 20)(
        half, total, far, top, bottom
    )[0]
    sent = late(halves[1:])
    got = lax.ppermute(sent, "core", [(0, 1), (1, 0)])
    kept = late(halves[:1])
    direct, mirror = call(
        spread, [shape((B, B), BF16), shape((8, 16, 2, 8, 128), BF16)], 0, 2, moved=3 << 20
    )(kept, got)
    direct = lax.ppermute(direct, ("core", "rep"), [(0, 0), (1, 2), (2, 1), (3, 3)])
    mirror = lax.all_to_all(mirror.reshape(256, 8, 128), AXES, split_axis=0, concat_axis=0, tiled=True)
    out = call(finish, [shape((B, B), F32)], 0, 2, moved=2 << 20)(direct, mirror.reshape(8, 8, 2, 2, 8, 128))[0]
    return out.reshape(16, 1, 32, B)


def solution(mesh):
    fine = Mesh(np.asarray(mesh.devices).reshape(8, 2, 4, 2, 2), AXES)
    block = P("row", ("xh", "y", "core"))
    out = P(None, ("xh", "y", "core"), None, ("row", "rep"))
    return jax.shard_map(local, mesh=fine, in_specs=(block, block), out_specs=out, check_vma=False)
```

```python
import functools

import jax
import jax.numpy as jnp
import numpy as np
from jax import lax
from jax.experimental import pallas as pl
from jax.experimental.pallas import tpu as pltpu
from jax.sharding import Mesh, PartitionSpec as P

AXES = ("row", "xh", "y", "core", "rep")
F32, BF16 = jnp.float32, jnp.bfloat16
X_LINE = ("xh", "rep")
PAIR = [(0, 1), (1, 0), (2, 3), (3, 2)]
CROSS = [(0, 3), (3, 0), (1, 2), (2, 1)]
COVER = 2**34
B = 512


def call(body, outs, n_scalar, n_in, flops=0, moved=0, scratch=(), limit=20, aliases={}):
    vmem = pl.BlockSpec(memory_space=pltpu.VMEM)
    smem = pl.BlockSpec(memory_space=pltpu.SMEM)
    return pl.pallas_call(
        body,
        out_shape=outs,
        in_specs=[smem] * n_scalar + [vmem] * n_in,
        out_specs=[vmem] * len(outs),
        scratch_shapes=list(scratch),
        input_output_aliases=aliases,
        compiler_params=pltpu.CompilerParams(vmem_limit_bytes=limit << 20),
        cost_estimate=pl.CostEstimate(flops=flops, bytes_accessed=moved, transcendentals=0),
    )


def lane_block(shape):
    return lax.broadcasted_iota(jnp.int32, shape, len(shape) - 1) // 32


def turn(parts):
    block = lane_block(parts[0].shape)
    out = []
    for j in range(4):
        rolled = [pltpu.roll(p, ((i - j) * 32) % 128, 1) if i != j else p for i, p in enumerate(parts)]
        out.append(
            jnp.where(
                block < 2, jnp.where(block == 0, rolled[0], rolled[1]), jnp.where(block == 2, rolled[2], rolled[3])
            )
        )
    return out


def w_pack(rep_ref, w_ref, out_ref):
    rep = rep_ref[0]
    for half in range(2):
        for g in range(4):
            parts = []
            for hi in range(4):
                v = w_ref[half * B + hi * 128 : half * B + (hi + 1) * 128, g * 128 : (g + 1) * 128].astype(F32)
                parts.append(jnp.where(rep == 0, v, pltpu.roll(v, 96, 1)))
            turned = turn(parts)
            for j in (0, 2):
                out_ref[g * 2 + j // 2, half] = turned[j].astype(BF16)


def w_unpack(in_ref, out_ref):
    for g in range(4):
        turned = turn([in_ref[4 * g + j].astype(F32) for j in range(4)])
        for hi in range(4):
            out_ref[hi * 128 : (hi + 1) * 128, g * 128 : (g + 1) * 128] = turned[hi].astype(BF16)


def dot(a, b):
    return jnp.dot(a, b, preferred_element_type=F32)


def hold_first(own_ref, up_ref, down_ref, held_ref):
    held_ref[0] = own_ref[...]
    held_ref[1] = up_ref[...]
    held_ref[4] = jnp.zeros((B, B), BF16)
    held_ref[7] = down_ref[...]


def hold_more(step, up_ref, down_ref, _, held_ref):
    held_ref[step] = up_ref[...]
    held_ref[8 - step] = down_ref[...]


def product_early(pos_ref, *refs):
    held, pieces, (sum_ref, far_ref) = refs[0], refs[1:9], refs[9:]
    for rows in (slice(0, B), slice(B, 2 * B)):
        total = None
        for p in range(8):
            term = dot(pieces[p][rows], held[pos_ref[p]])
            total = term if total is None else total + term
        sum_ref[rows] = total
    for p in range(8):

        @pl.when(pos_ref[p] == 4)
        def _(p=p):
            far_ref[...] = pieces[p][...]


def product_late(half_ref, sum_ref, far_ref, top_ref, bottom_ref, out_ref):
    rows = pl.ds(pl.multiple_of(half_ref[0] * B, B), B)
    block = far_ref[rows, :]
    out_ref[...] = sum_ref[rows, :] + dot(block[:, : B // 2], top_ref[...]) + dot(block[:, B // 2 :], bottom_ref[...])


def spread(kept_ref, got_ref, direct_ref, mirror_ref):
    cycle = (kept_ref[...] + got_ref[...]).astype(BF16).astype(F32)
    direct_ref[...] = cycle.T.astype(BF16)
    split = cycle.reshape(16, 4, 8, B)
    for g in range(4):
        parts = [split[:, hi, :, g * 128 : (g + 1) * 128].reshape(128, 128) for hi in range(4)]
        for j, t in enumerate(turn(parts)):
            mirror_ref[2 * g + j // 2, :, j % 2] = t.reshape(16, 8, 128).astype(BF16)


def finish(direct_ref, mirror_ref, out_ref):
    for owner in range(16):
        z, core = owner // 2, owner % 2
        for g in range(4):
            parts = [mirror_ref[z, 2 * g + j // 2, core, j % 2].astype(F32) for j in range(4)]
            for hi, t in enumerate(turn(parts)):
                rows = slice(owner * 32 + hi * 8, owner * 32 + hi * 8 + 8)
                lanes = slice(g * 128, (g + 1) * 128)
                out_ref[rows, lanes] = t + direct_ref[rows, lanes].astype(F32)


def ring(n, step):
    return [(i, (i + step) % n) for i in range(n)]


def along_y(v):
    perm = []
    for y in range(4):
        for core in range(2):
            for rep in range(2):
                to = (y + (1 if core ^ rep else -1)) % 4
                perm.append(((y * 2 + core) * 2 + rep, (to * 2 + core) * 2 + rep))
    return lax.ppermute(v, ("y", "core", "rep"), perm)


def local(amplitudes, intermediate):
    z, xh, y, core, rep = (lax.axis_index(a) for a in AXES)
    shape = jax.ShapeDtypeStruct
    pair = lambda v: lax.ppermute(v, X_LINE, PAIR)
    cross = lambda v: lax.ppermute(v, X_LINE, CROSS)
    above = lambda v: lax.ppermute(v, "row", ring(8, -1))
    below = lambda v: lax.ppermute(v, "row", ring(8, 1))

    step = 1 - 2 * (core ^ rep)
    position = jnp.stack(
        [(4 * ((xh + i) % 2) + (y + j + 4) % 4 - z + 8) % 8 for i in range(2) for j in (0, step, 2, -step)]
    ).astype(jnp.int32)
    halves = jnp.stack([core, 1 - core]).astype(jnp.int32)
    rep = rep.reshape(1).astype(jnp.int32)
    position, halves, rep, intermediate, own = lax.optimization_barrier(
        (position, halves, rep, intermediate, amplitudes)
    )

    packed = call(w_pack, [shape((8, 2, 128, 128), BF16)], 1, 1, moved=2 << 20)(rep, intermediate)[0]
    arrived = lax.all_to_all(packed.reshape(16, 128, 128), ("xh", "y", "core"), split_axis=0, concat_axis=0, tiled=True)
    w0 = call(w_unpack, [shape((B, B), BF16)], 0, 1, moved=1 << 20)(arrived)[0]

    y1, c1_top = along_y(own), cross(own[:B])
    w0, y1, c1_top = lax.optimization_barrier((w0, y1, c1_top))
    w1, w7 = above(w0), below(w0)
    y2, p1, c1_bottom = along_y(y1), pair(y1), cross(own[B:])

    stack = call(hold_first, [shape((8, B, B), BF16)], 0, 3, flops=COVER)(w0, w1, w7)[0]
    y2, c1_bottom, y1, _ = lax.optimization_barrier((y2, c1_bottom, y1, w1))
    c1 = jnp.concatenate([c1_top, c1_bottom])
    w2, w6 = above(w1), below(w7)
    y3, c2 = along_y(c1), cross(y1)

    more = lambda step, cover, *chunks: call(
        functools.partial(hold_more, step), [shape((8, B, B), BF16)], 0, 3, flops=cover, aliases={2: 0}
    )(*chunks)[0]
    stack = more(2, COVER, w2, w6, stack)
    y3, p1, _ = lax.optimization_barrier((y3, p1, w2))
    w3, w5 = above(w2), below(w6)
    y4 = along_y(y3)

    stack = more(3, 0, w3, w5, stack)
    top, bottom = above(w3[: B // 2]), below(w5[B // 2 :])

    total, far = call(
        product_early,
        [shape((2 * B, B), F32), shape((2 * B, B), BF16)],
        1,
        9,
        flops=32 * B**3,
        moved=16 << 20,
        limit=28,
    )(position, stack, own, y1, y2, p1, c1, y3, y4, c2)
    late = lambda half: call(product_late, [shape((B, B), F32)], 1, 4, flops=2 * B**3, moved=4 << 20)(
        half, total, far, top, bottom
    )[0]
    sent = late(halves[1:])
    got = lax.ppermute(sent, "core", [(0, 1), (1, 0)])
    kept = late(halves[:1])
    direct, mirror = call(
        spread, [shape((B, B), BF16), shape((8, 16, 2, 8, 128), BF16)], 0, 2, moved=3 << 20
    )(kept, got)
    direct = lax.ppermute(direct, ("core", "rep"), [(0, 0), (1, 2), (2, 1), (3, 3)])
    mirror = lax.all_to_all(mirror.reshape(256, 8, 128), AXES, split_axis=0, concat_axis=0, tiled=True)
    out = call(finish, [shape((B, B), F32)], 0, 2, moved=2 << 20)(direct, mirror.reshape(8, 8, 2, 2, 8, 128))[0]
    return out.reshape(16, 1, 32, B)


def solution(mesh):
    fine = Mesh(np.asarray(mesh.devices).reshape(8, 2, 4, 2, 2), AXES)
    block = P("row", ("xh", "y", "core"))
    out = P(None, ("xh", "y", "core"), None, ("row", "rep"))
    return jax.shard_map(local, mesh=fine, in_specs=(block, block), out_specs=out, check_vma=False)
```

```python
import functools

import jax
import jax.numpy as jnp
import numpy as np
from jax import lax
from jax.experimental import pallas as pl
from jax.experimental.pallas import tpu as pltpu
from jax.sharding import Mesh, PartitionSpec as P

AXES = ("row", "xh", "y", "core", "rep")
F32, BF16 = jnp.float32, jnp.bfloat16
X_LINE = ("xh", "rep")
PAIR = [(0, 1), (1, 0), (2, 3), (3, 2)]
CROSS = [(0, 3), (3, 0), (1, 2), (2, 1)]
COVER = 2**34
B = 512


def call(body, outs, n_scalar, n_in, flops=0, moved=0, scratch=(), limit=20, aliases={}):
    vmem = pl.BlockSpec(memory_space=pltpu.VMEM)
    smem = pl.BlockSpec(memory_space=pltpu.SMEM)
    return pl.pallas_call(
        body,
        out_shape=outs,
        in_specs=[smem] * n_scalar + [vmem] * n_in,
        out_specs=[vmem] * len(outs),
        scratch_shapes=list(scratch),
        input_output_aliases=aliases,
        compiler_params=pltpu.CompilerParams(vmem_limit_bytes=limit << 20),
        cost_estimate=pl.CostEstimate(flops=flops, bytes_accessed=moved, transcendentals=0),
    )


def lane_block(shape):
    return lax.broadcasted_iota(jnp.int32, shape, len(shape) - 1) // 32


def turn(parts):
    block = lane_block(parts[0].shape)
    out = []
    for j in range(4):
        rolled = [pltpu.roll(p, ((i - j) * 32) % 128, 1) if i != j else p for i, p in enumerate(parts)]
        out.append(
            jnp.where(
                block < 2, jnp.where(block == 0, rolled[0], rolled[1]), jnp.where(block == 2, rolled[2], rolled[3])
            )
        )
    return out


def w_pack(rep_ref, w_ref, out_ref):
    rep = rep_ref[0]
    for half in range(2):
        for g in range(4):
            parts = []
            for hi in range(4):
                v = w_ref[half * B + hi * 128 : half * B + (hi + 1) * 128, g * 128 : (g + 1) * 128].astype(F32)
                parts.append(jnp.where(rep == 0, v, pltpu.roll(v, 96, 1)))
            turned = turn(parts)
            for j in (0, 2):
                out_ref[g * 2 + j // 2, half] = turned[j].astype(BF16)


def w_unpack(in_ref, out_ref):
    for g in range(4):
        turned = turn([in_ref[4 * g + j].astype(F32) for j in range(4)])
        for hi in range(4):
            out_ref[hi * 128 : (hi + 1) * 128, g * 128 : (g + 1) * 128] = turned[hi].astype(BF16)


def dot(a, b):
    return jnp.dot(a, b, preferred_element_type=F32)


def hold_first(own_ref, up_ref, down_ref, held_ref):
    held_ref[0] = own_ref[...]
    held_ref[1] = up_ref[...]
    held_ref[4] = jnp.zeros((B, B), BF16)
    held_ref[7] = down_ref[...]


def hold_more(step, up_ref, down_ref, _, held_ref):
    held_ref[step] = up_ref[...]
    held_ref[8 - step] = down_ref[...]


def product_early(pos_ref, *refs):
    held, pieces, (sum_ref, far_ref) = refs[0], refs[1:9], refs[9:]
    for rows in (slice(0, B), slice(B, 2 * B)):
        total = None
        for p in range(8):
            term = dot(pieces[p][rows], held[pos_ref[p]])
            total = term if total is None else total + term
        sum_ref[rows] = total
    for p in range(8):

        @pl.when(pos_ref[p] == 4)
        def _(p=p):
            far_ref[...] = pieces[p][...]


def product_late(half_ref, sum_ref, far_ref, top_ref, bottom_ref, out_ref):
    rows = pl.ds(pl.multiple_of(half_ref[0] * B, B), B)
    block = far_ref[rows, :]
    out_ref[...] = sum_ref[rows, :] + dot(block[:, : B // 2], top_ref[...]) + dot(block[:, B // 2 :], bottom_ref[...])


def mirrored(kept_ref, got_ref, mirror_ref):
    cycle = (kept_ref[...] + got_ref[...]).astype(BF16).astype(F32)
    split = cycle.reshape(16, 4, 8, B)
    for g in range(4):
        parts = [split[:, hi, :, g * 128 : (g + 1) * 128].reshape(128, 128) for hi in range(4)]
        for j, t in enumerate(turn(parts)):
            mirror_ref[2 * g + j // 2, :, j % 2] = t.reshape(16, 8, 128).astype(BF16)


def transposed(kept_ref, got_ref, _, direct_ref):
    cycle = (kept_ref[...] + got_ref[...]).astype(BF16).astype(F32)
    direct_ref[...] = cycle.T.astype(BF16)


def finish(direct_ref, mirror_ref, out_ref):
    for owner in range(16):
        z, core = owner // 2, owner % 2
        for g in range(4):
            parts = [mirror_ref[z, 2 * g + j // 2, core, j % 2].astype(F32) for j in range(4)]
            for hi, t in enumerate(turn(parts)):
                rows = slice(owner * 32 + hi * 8, owner * 32 + hi * 8 + 8)
                lanes = slice(g * 128, (g + 1) * 128)
                out_ref[rows, lanes] = t + direct_ref[rows, lanes].astype(F32)


def ring(n, step):
    return [(i, (i + step) % n) for i in range(n)]


def along_y(v):
    perm = []
    for y in range(4):
        for core in range(2):
            for rep in range(2):
                to = (y + (1 if core ^ rep else -1)) % 4
                perm.append(((y * 2 + core) * 2 + rep, (to * 2 + core) * 2 + rep))
    return lax.ppermute(v, ("y", "core", "rep"), perm)


def local(amplitudes, intermediate):
    z, xh, y, core, rep = (lax.axis_index(a) for a in AXES)
    shape = jax.ShapeDtypeStruct
    pair = lambda v: lax.ppermute(v, X_LINE, PAIR)
    cross = lambda v: lax.ppermute(v, X_LINE, CROSS)
    above = lambda v: lax.ppermute(v, "row", ring(8, -1))
    below = lambda v: lax.ppermute(v, "row", ring(8, 1))

    step = 1 - 2 * (core ^ rep)
    position = jnp.stack(
        [(4 * ((xh + i) % 2) + (y + j + 4) % 4 - z + 8) % 8 for i in range(2) for j in (0, step, 2, -step)]
    ).astype(jnp.int32)
    halves = jnp.stack([core, 1 - core]).astype(jnp.int32)
    rep = rep.reshape(1).astype(jnp.int32)
    position, halves, rep, intermediate, own = lax.optimization_barrier(
        (position, halves, rep, intermediate, amplitudes)
    )

    packed = call(w_pack, [shape((8, 2, 128, 128), BF16)], 1, 1, moved=2 << 20)(rep, intermediate)[0]
    arrived = lax.all_to_all(packed.reshape(16, 128, 128), ("xh", "y", "core"), split_axis=0, concat_axis=0, tiled=True)
    w0 = call(w_unpack, [shape((B, B), BF16)], 0, 1, moved=1 << 20)(arrived)[0]

    y1, c1_top = along_y(own), cross(own[:B])
    w0, y1, c1_top = lax.optimization_barrier((w0, y1, c1_top))
    w1, w7 = above(w0), below(w0)
    y2, p1, c1_bottom = along_y(y1), pair(y1), cross(own[B:])

    stack = call(hold_first, [shape((8, B, B), BF16)], 0, 3, flops=COVER)(w0, w1, w7)[0]
    y2, c1_bottom, y1, _ = lax.optimization_barrier((y2, c1_bottom, y1, w1))
    c1 = jnp.concatenate([c1_top, c1_bottom])
    w2, w6 = above(w1), below(w7)
    y3, c2 = along_y(c1), cross(y1)

    more = lambda step, cover, *chunks: call(
        functools.partial(hold_more, step), [shape((8, B, B), BF16)], 0, 3, flops=cover, aliases={2: 0}
    )(*chunks)[0]
    stack = more(2, COVER, w2, w6, stack)
    y3, p1, _ = lax.optimization_barrier((y3, p1, w2))
    w3, w5 = above(w2), below(w6)
    y4 = along_y(y3)

    stack = more(3, 0, w3, w5, stack)
    top, bottom = above(w3[: B // 2]), below(w5[B // 2 :])

    total, far = call(
        product_early,
        [shape((2 * B, B), F32), shape((2 * B, B), BF16)],
        1,
        9,
        flops=32 * B**3,
        moved=16 << 20,
        limit=28,
    )(position, stack, own, y1, y2, p1, c1, y3, y4, c2)
    late = lambda half: call(product_late, [shape((B, B), F32)], 1, 4, flops=2 * B**3, moved=4 << 20)(
        half, total, far, top, bottom
    )[0]
    sent = late(halves[1:])
    got = lax.ppermute(sent, "core", [(0, 1), (1, 0)])
    kept = late(halves[:1])
    mirror = call(mirrored, [shape((8, 16, 2, 8, 128), BF16)], 0, 2, moved=3 << 20)(kept, got)[0]
    direct = pl.pallas_call(
        transposed,
        out_shape=shape((B, B), BF16),
        in_specs=[pl.BlockSpec(memory_space=pltpu.VMEM)] * 2 + [pl.BlockSpec(memory_space=pl.ANY)],
        out_specs=pl.BlockSpec(memory_space=pltpu.VMEM),
        compiler_params=pltpu.CompilerParams(vmem_limit_bytes=20 << 20),
        cost_estimate=pl.CostEstimate(flops=0, bytes_accessed=3 << 20, transcendentals=0),
    )(kept, got, mirror)
    direct = lax.ppermute(direct, ("core", "rep"), [(0, 0), (1, 2), (2, 1), (3, 3)])
    mirror = lax.all_to_all(mirror.reshape(256, 8, 128), AXES, split_axis=0, concat_axis=0, tiled=True)
    out = call(finish, [shape((B, B), F32)], 0, 2, moved=2 << 20)(direct, mirror.reshape(8, 8, 2, 2, 8, 128))[0]
    return out.reshape(16, 1, 32, B)


def solution(mesh):
    fine = Mesh(np.asarray(mesh.devices).reshape(8, 2, 4, 2, 2), AXES)
    block = P("row", ("xh", "y", "core"))
    out = P(None, ("xh", "y", "core"), None, ("row", "rep"))
    return jax.shard_map(local, mesh=fine, in_specs=(block, block), out_specs=out, check_vma=False)
```

```python
import functools

import jax
import jax.numpy as jnp
import numpy as np
from jax import lax
from jax.experimental import pallas as pl
from jax.experimental.pallas import tpu as pltpu
from jax.sharding import Mesh, PartitionSpec as P

AXES = ("row", "xh", "y", "core", "rep")
F32, BF16 = jnp.float32, jnp.bfloat16
X_LINE = ("xh", "rep")
PAIR = [(0, 1), (1, 0), (2, 3), (3, 2)]
CROSS = [(0, 3), (3, 0), (1, 2), (2, 1)]
COVER = 2**34
B = 512


def call(body, outs, n_scalar, n_in, flops=0, moved=0, scratch=(), limit=20, aliases={}):
    vmem = pl.BlockSpec(memory_space=pltpu.VMEM)
    smem = pl.BlockSpec(memory_space=pltpu.SMEM)
    return pl.pallas_call(
        body,
        out_shape=outs,
        in_specs=[smem] * n_scalar + [vmem] * n_in,
        out_specs=[vmem] * len(outs),
        scratch_shapes=list(scratch),
        input_output_aliases=aliases,
        compiler_params=pltpu.CompilerParams(vmem_limit_bytes=limit << 20),
        cost_estimate=pl.CostEstimate(flops=flops, bytes_accessed=moved, transcendentals=0),
    )


def lane_block(shape):
    return lax.broadcasted_iota(jnp.int32, shape, len(shape) - 1) // 32


def turn(parts):
    block = lane_block(parts[0].shape)
    out = []
    for j in range(4):
        rolled = [pltpu.roll(p, ((i - j) * 32) % 128, 1) if i != j else p for i, p in enumerate(parts)]
        out.append(
            jnp.where(
                block < 2, jnp.where(block == 0, rolled[0], rolled[1]), jnp.where(block == 2, rolled[2], rolled[3])
            )
        )
    return out


def w_pack(rep_ref, w_ref, out_ref):
    rep = rep_ref[0]
    for g in range(4):
        parts = []
        for hi in range(4):
            v = w_ref[hi * 128 : (hi + 1) * 128, g * 128 : (g + 1) * 128].astype(F32)
            parts.append(jnp.where(rep == 0, v, pltpu.roll(v, 96, 1)))
        turned = turn(parts)
        for j in (0, 2):
            out_ref[g * 2 + j // 2, 0] = turned[j].astype(BF16)


def w_unpack(in_ref, out_ref):
    for g in range(4):
        turned = turn([in_ref[4 * g + j].astype(F32) for j in range(4)])
        for hi in range(4):
            out_ref[hi * 128 : (hi + 1) * 128, g * 128 : (g + 1) * 128] = turned[hi].astype(BF16)


def dot(a, b):
    return jnp.dot(a, b, preferred_element_type=F32)


def hold_first(own_ref, up_ref, down_ref, held_ref):
    held_ref[0] = own_ref[...]
    held_ref[1] = up_ref[...]
    held_ref[4] = jnp.zeros((B, B), BF16)
    held_ref[7] = down_ref[...]


def hold_more(step, up_ref, down_ref, _, held_ref):
    held_ref[step] = up_ref[...]
    held_ref[8 - step] = down_ref[...]


def product_early(pos_ref, *refs):
    held, pieces, (sum_ref, far_ref) = refs[0], refs[1:9], refs[9:]
    for rows in (slice(0, B), slice(B, 2 * B)):
        total = None
        for p in range(8):
            term = dot(pieces[p][rows], held[pos_ref[p]])
            total = term if total is None else total + term
        sum_ref[rows] = total
    for p in range(8):

        @pl.when(pos_ref[p] == 4)
        def _(p=p):
            far_ref[...] = pieces[p][...]


def product_late(half_ref, sum_ref, far_ref, top_ref, bottom_ref, out_ref):
    rows = pl.ds(pl.multiple_of(half_ref[0] * B, B), B)
    block = far_ref[rows, :]
    out_ref[...] = sum_ref[rows, :] + dot(block[:, : B // 2], top_ref[...]) + dot(block[:, B // 2 :], bottom_ref[...])


def mirrored(kept_ref, got_ref, mirror_ref):
    cycle = (kept_ref[...] + got_ref[...]).astype(BF16).astype(F32)
    split = cycle.reshape(16, 4, 8, B)
    for g in range(4):
        parts = [split[:, hi, :, g * 128 : (g + 1) * 128].reshape(128, 128) for hi in range(4)]
        for j, t in enumerate(turn(parts)):
            mirror_ref[2 * g + j // 2, :, j % 2] = t.reshape(16, 8, 128).astype(BF16)


def transposed(kept_ref, got_ref, _, direct_ref):
    cycle = (kept_ref[...] + got_ref[...]).astype(BF16).astype(F32)
    direct_ref[...] = cycle.T.astype(BF16)


def finish(direct_ref, mirror_ref, out_ref):
    for owner in range(16):
        z, core = owner // 2, owner % 2
        for g in range(4):
            parts = [mirror_ref[z, 2 * g + j // 2, core, j % 2].astype(F32) for j in range(4)]
            for hi, t in enumerate(turn(parts)):
                rows = slice(owner * 32 + hi * 8, owner * 32 + hi * 8 + 8)
                lanes = slice(g * 128, (g + 1) * 128)
                out_ref[rows, lanes] = t + direct_ref[rows, lanes].astype(F32)


def ring(n, step):
    return [(i, (i + step) % n) for i in range(n)]


def along_y(v):
    perm = []
    for y in range(4):
        for core in range(2):
            for rep in range(2):
                to = (y + (1 if core ^ rep else -1)) % 4
                perm.append(((y * 2 + core) * 2 + rep, (to * 2 + core) * 2 + rep))
    return lax.ppermute(v, ("y", "core", "rep"), perm)


def local(amplitudes, intermediate):
    z, xh, y, core, rep = (lax.axis_index(a) for a in AXES)
    shape = jax.ShapeDtypeStruct
    pair = lambda v: lax.ppermute(v, X_LINE, PAIR)
    cross = lambda v: lax.ppermute(v, X_LINE, CROSS)
    above = lambda v: lax.ppermute(v, "row", ring(8, -1))
    below = lambda v: lax.ppermute(v, "row", ring(8, 1))

    step = 1 - 2 * (core ^ rep)
    position = jnp.stack(
        [(4 * ((xh + i) % 2) + (y + j + 4) % 4 - z + 8) % 8 for i in range(2) for j in (0, step, 2, -step)]
    ).astype(jnp.int32)
    halves = jnp.stack([core, 1 - core]).astype(jnp.int32)
    rep = rep.reshape(1).astype(jnp.int32)
    position, halves, rep, intermediate, own = lax.optimization_barrier(
        (position, halves, rep, intermediate, amplitudes)
    )

    packed = pl.pallas_call(
        w_pack,
        out_shape=shape((8, 2, 128, 128), BF16),
        grid=(2,),
        in_specs=[pl.BlockSpec(memory_space=pltpu.SMEM), pl.BlockSpec((B, B), lambda i: (i, 0))],
        out_specs=pl.BlockSpec((8, 1, 128, 128), lambda i: (0, i, 0, 0)),
        compiler_params=pltpu.CompilerParams(vmem_limit_bytes=20 << 20),
        cost_estimate=pl.CostEstimate(flops=0, bytes_accessed=2 << 20, transcendentals=0),
    )(rep, intermediate)
    arrived = lax.all_to_all(packed.reshape(16, 128, 128), ("xh", "y", "core"), split_axis=0, concat_axis=0, tiled=True)
    w0 = call(w_unpack, [shape((B, B), BF16)], 0, 1, moved=1 << 20)(arrived)[0]

    y1, c1_top = along_y(own), cross(own[:B])
    w0, y1, c1_top = lax.optimization_barrier((w0, y1, c1_top))
    w1, w7 = above(w0), below(w0)
    y2, p1, c1_bottom = along_y(y1), pair(y1), cross(own[B:])

    stack = call(hold_first, [shape((8, B, B), BF16)], 0, 3, flops=COVER)(w0, w1, w7)[0]
    y2, c1_bottom, y1, _ = lax.optimization_barrier((y2, c1_bottom, y1, w1))
    c1 = jnp.concatenate([c1_top, c1_bottom])
    w2, w6 = above(w1), below(w7)
    y3, c2 = along_y(c1), cross(y1)

    more = lambda step, cover, *chunks: call(
        functools.partial(hold_more, step), [shape((8, B, B), BF16)], 0, 3, flops=cover, aliases={2: 0}
    )(*chunks)[0]
    stack = more(2, COVER, w2, w6, stack)
    y3, p1, _ = lax.optimization_barrier((y3, p1, w2))
    w3, w5 = above(w2), below(w6)
    y4 = along_y(y3)

    stack = more(3, 0, w3, w5, stack)
    top, bottom = above(w3[: B // 2]), below(w5[B // 2 :])

    total, far = call(
        product_early,
        [shape((2 * B, B), F32), shape((2 * B, B), BF16)],
        1,
        9,
        flops=32 * B**3,
        moved=16 << 20,
        limit=28,
    )(position, stack, own, y1, y2, p1, c1, y3, y4, c2)
    late = lambda half: call(product_late, [shape((B, B), F32)], 1, 4, flops=2 * B**3, moved=4 << 20)(
        half, total, far, top, bottom
    )[0]
    sent = late(halves[1:])
    got = lax.ppermute(sent, "core", [(0, 1), (1, 0)])
    kept = late(halves[:1])
    mirror = call(mirrored, [shape((8, 16, 2, 8, 128), BF16)], 0, 2, moved=3 << 20)(kept, got)[0]
    direct = pl.pallas_call(
        transposed,
        out_shape=shape((B, B), BF16),
        in_specs=[pl.BlockSpec(memory_space=pltpu.VMEM)] * 2 + [pl.BlockSpec(memory_space=pl.ANY)],
        out_specs=pl.BlockSpec(memory_space=pltpu.VMEM),
        compiler_params=pltpu.CompilerParams(vmem_limit_bytes=20 << 20),
        cost_estimate=pl.CostEstimate(flops=0, bytes_accessed=3 << 20, transcendentals=0),
    )(kept, got, mirror)
    direct = lax.ppermute(direct, ("core", "rep"), [(0, 0), (1, 2), (2, 1), (3, 3)])
    mirror = lax.all_to_all(mirror.reshape(256, 8, 128), AXES, split_axis=0, concat_axis=0, tiled=True)
    out = call(finish, [shape((B, B), F32)], 0, 2, moved=2 << 20)(direct, mirror.reshape(8, 8, 2, 2, 8, 128))[0]
    return out.reshape(16, 1, 32, B)


def solution(mesh):
    fine = Mesh(np.asarray(mesh.devices).reshape(8, 2, 4, 2, 2), AXES)
    block = P("row", ("xh", "y", "core"))
    out = P(None, ("xh", "y", "core"), None, ("row", "rep"))
    return jax.shard_map(local, mesh=fine, in_specs=(block, block), out_specs=out, check_vma=False)
```
